32 devices in a mesh: dp: 2 (over x), row: 4 (over z), col: 4 (over y, core).
Axes of the slice: x: 2, y: 2, z: 4, core: 2. Of those that a mesh axis runs over, the one named last changes fastest.
Arguments:
- hidden_in: bfloat16 [4096, 1024], P(('dp', 'row'), 'col'), may hold values from -18 to 18
- doc_ids: int32 [8, 512], P(('dp', 'row')), may hold values from 0 to 3, as said below
- w_qkv: bfloat16 [1024, 3, 1024], P('row', None, 'col'), may hold values from -0.1875 to 0.1875
- query_bias: float32 [1024], P('col'), may hold values from -3 to 3
- value_bias: float32 [1024], P('col'), may hold values from -3 to 3
- w_out: bfloat16 [1024, 1024], P('col', 'row'), may hold values from -0.75 to 0.75
- out_bias: float32 [1024], P('col'), may hold values from -3 to 3
- norm_gain: float32 [1024], P('col'), may hold values from 0.5 to 1.5
- norm_shift: float32 [1024], P('col'), may hold values from -3 to 3
- w_up: bfloat16 [1024, 4096], P('row', 'col'), may hold values from -0.1875 to 0.1875
- up_bias: float32 [4096], P('col'), may hold values from -3 to 3
- w_down: bfloat16 [4096, 1024], P('col', 'row'), may hold values from -0.09375 to 0.09375
- down_bias: float32 [1024], P('col'), may hold values from -3 to 3
- final_gain: float32 [1024], P('col'), may hold values from 0.5 to 1.5
- final_shift: float32 [1024], P('col'), may hold values from -3 to 3
- out_grad: bfloat16 [4096, 1024], P(('dp', 'row'), 'col'), may hold values from -6 to 6
Outputs:
- layer_out: bfloat16 [4096, 1024], P(('dp', 'row'), 'col')
- hidden_grad: float32 [4096, 1024], P(('dp', 'row'), 'col')
- wqkv_grad: float32 [1024, 3, 1024], P('row', None, 'col')
- qbias_grad: float32 [1024], P('col')
- vbias_grad: float32 [1024], P('col')
- wout_grad: float32 [1024, 1024], P('col', 'row')
- obias_grad: float32 [1024], P('col')
- ngain_grad: float32 [1024], P('col')
- nshift_grad: float32 [1024], P('col')
- wup_grad: float32 [1024, 4096], P('row', 'col')
- ubias_grad: float32 [4096], P('col')
- wdown_grad: float32 [4096, 1024], P('col', 'row')
- dbias_grad: float32 [1024], P('col')
- fgain_grad: float32 [1024], P('col')
- fshift_grad: float32 [1024], P('col')
The draws below stay inside these ranges and needn't reach their ends.
Inputs may be any that keep to these rules, and one draw needn't show every extreme that they name: `doc_ids`: along each sequence the ids never fall, start at 0 and end at 3: every sequence packs four documents, each of 51 tokens or more.
All inputs are finite; a program needn't handle non-finite values.
Results may differ from the reference program's by a relative error of at most 0.015.
Values may be sent and summed in bfloat16 or wider, within the bound.
A program may use at most 128 MiB of HBM per device.

```python
import math
import jax
import jax.numpy as jnp
from jax import lax

D = 1024
FF = 4096
HEADS = 16
HD = 64
LEN = 512
SEQS = 8
TOKENS = 4096


def draw_hidden_in(key, part):
    k_col, k_base = jax.random.split(key, 2)
    feature = jnp.arange(D, dtype=jnp.float32) / D
    columns = 0.3 * 10.0 ** (0.5 * feature + 0.5 * jax.random.uniform(k_col, (D,), dtype=jnp.float32))
    base = jnp.clip(jax.random.normal(k_base, (TOKENS, D), dtype=jnp.float32), -6.0, 6.0) * columns
    return jnp.clip(base, -18.0, 18.0).astype(jnp.bfloat16)


def draw_doc_ids(key, part):
    min_doc = LEN // 10
    room = LEN - 4 * min_doc
    seq_keys = jax.random.split(key, SEQS)
    picks = jax.vmap(lambda single: jnp.sort(jax.random.permutation(single, room + 3)[:3]))(seq_keys)
    steps_int = jnp.arange(3, dtype=jnp.int32)
    breaks = (picks.astype(jnp.int32) - steps_int[None, :] + (steps_int[None, :] + 1) * min_doc).astype(jnp.int32)
    position = jnp.arange(LEN, dtype=jnp.int32)
    return jnp.sum((position[None, :, None] >= breaks[:, None, :]).astype(jnp.int32), axis=-1).astype(jnp.int32)


def draw_w_qkv(key, part):
    k_query, k_key, k_value = jax.random.split(key, 3)
    narrow = D ** (-0.5)
    w_query = jnp.clip(jax.random.normal(k_query, (D, D), dtype=jnp.float32), -6.0, 6.0) * narrow
    fresh = jnp.clip(jax.random.normal(k_key, (D, D), dtype=jnp.float32), -6.0, 6.0) * narrow
    w_key = fresh
    w_value = jnp.clip(jax.random.normal(k_value, (D, D), dtype=jnp.float32), -6.0, 6.0) * narrow
    return jnp.stack([w_query, w_key, w_value], axis=1).astype(jnp.bfloat16)


def shard_levels(key, shape, cuts, smallest, high):
    def one(dim, parts):
        heights = jax.random.uniform(jax.random.fold_in(jax.random.fold_in(key, 6), dim), (parts,), jnp.float32, smallest / len(cuts), high / len(cuts))
        return jnp.repeat(jnp.exp(heights), shape[dim] // parts).reshape((-1,) + (1,) * (len(shape) - dim - 1))

    factor_of = one(*cuts[0])
    for cut in cuts[1:]:
        factor_of = factor_of * one(*cut)
    return factor_of


def noise(key, dims, deviation, reach, pieces=(), held_as=jnp.bfloat16):
    values = jax.random.normal(key, dims, jnp.float32) * deviation
    if len(pieces) > 0:
        values = shard_levels(key, dims, pieces, -0.22, 0.18) * values
    return jnp.clip(values, min=-reach, max=reach).astype(held_as)


def setup_inputs(seed: int = 0) -> dict:
    streams_of = jax.random.split(jax.random.key(seed), 17)
    return {
        "hidden_in": draw_hidden_in(jax.random.fold_in(streams_of[16], 71), 0),
        "doc_ids": draw_doc_ids(jax.random.fold_in(streams_of[16], 71), 0),
        "w_qkv": draw_w_qkv(jax.random.fold_in(streams_of[16], 71), 0),
        "query_bias": noise(streams_of[3], (D,), 0.5, 3.0, ((0, 4),), jnp.float32),
        "value_bias": noise(streams_of[4], (D,), 0.5, 3.0, ((0, 4),), jnp.float32),
        "w_out": noise(streams_of[5], (D, D), (D // 16) ** -0.5, 0.75, ((0, 4), (1, 4))),
        "out_bias": noise(streams_of[6], (D,), 0.5, 3.0, ((0, 4),), jnp.float32),
        "norm_gain": jnp.clip(1.0 + 0.1 * jax.random.normal(streams_of[7], (D,), jnp.float32), 0.5, 1.5),
        "norm_shift": noise(streams_of[8], (D,), 0.5, 3.0, ((0, 4),), jnp.float32),
        "w_up": noise(streams_of[9], (D, FF), D ** -0.5, 0.1875, ((0, 4), (1, 4))),
        "up_bias": noise(streams_of[10], (FF,), 0.5, 3.0, ((0, 4),), jnp.float32),
        "w_down": noise(streams_of[11], (FF, D), FF ** -0.5, 0.09375, ((0, 4), (1, 4))),
        "down_bias": noise(streams_of[12], (D,), 0.5, 3.0, ((0, 4),), jnp.float32),
        "final_gain": jnp.clip(1.0 + 0.1 * jax.random.normal(streams_of[13], (D,), jnp.float32), 0.5, 1.5),
        "final_shift": noise(streams_of[14], (D,), 0.5, 3.0, ((0, 4),), jnp.float32),
        "out_grad": noise(streams_of[15], (TOKENS, D), 1.0, 6.0, ((0, 8), (1, 4))),
    }


EPS = 1e-12
INV_ROOT_TWO = 0.7071067811865476
INV_ROOT_PI = 0.3989422804014327

def rounded(values_in):
    return lax.optimization_barrier(values_in.astype(jnp.bfloat16))

def gelu_parts(pre_act):
    cdf_val = 0.5 * (1.0 + lax.erf(pre_act * INV_ROOT_TWO))
    density = jnp.exp(-0.5 * pre_act * pre_act) * INV_ROOT_PI
    return (pre_act * cdf_val, cdf_val + pre_act * density)

def norm_fwd(total, gain, shift):
    mean_val = lax.optimization_barrier(jnp.mean(total, axis=-1, keepdims=True))
    centered = total - mean_val
    variance = lax.optimization_barrier(jnp.mean(centered * centered, axis=-1, keepdims=True))
    inverse = lax.rsqrt(variance + EPS)
    normed = centered * inverse
    return (normed * gain + shift, normed, inverse)

def norm_bwd(upstream, normed, inverse, gain):
    scaled = upstream * gain
    first_mean = lax.optimization_barrier(jnp.mean(scaled, axis=-1, keepdims=True))
    second_mean = lax.optimization_barrier(jnp.mean(scaled * normed, axis=-1, keepdims=True))
    return inverse * (scaled - first_mean - normed * second_mean)

def reference(hidden_in, doc_ids, w_qkv, query_bias, value_bias, w_out, out_bias, norm_gain, norm_shift, w_up, up_bias, w_down, down_bias, final_gain, final_shift, out_grad):
    group_seqs = math.gcd(SEQS, 8)
    block_count = SEQS // group_seqs
    block_rows = group_seqs * LEN
    wq_flat = w_qkv.reshape(D, 3 * D)
    score_scale = HD ** (-0.5)
    f32 = jnp.float32

    def block_step(running, block_in):
        x_block, id_block, g_block = block_in
        projected = jnp.dot(x_block, wq_flat, preferred_element_type=f32).reshape(block_rows, 3, D)
        query = rounded(projected[:, 0] + query_bias).reshape(group_seqs, LEN, HEADS, HD)
        keys = rounded(projected[:, 1]).reshape(group_seqs, LEN, HEADS, HD)
        values = rounded(projected[:, 2] + value_bias).reshape(group_seqs, LEN, HEADS, HD)
        same_doc = (id_block[:, :, None] == id_block[:, None, :])[:, None]
        scores = jnp.einsum('bqhd,bkhd->bhqk', query.astype(f32), keys.astype(f32)) * score_scale
        scores = jnp.where(same_doc, scores, -jnp.inf)
        top_score = lax.optimization_barrier(jnp.max(scores, axis=-1, keepdims=True))
        log_total = top_score + jnp.log(lax.optimization_barrier(jnp.sum(jnp.exp(scores - top_score), axis=-1, keepdims=True)))
        prob_f = jnp.exp(scores - log_total)
        prob_bf = rounded(prob_f)
        context = rounded(jnp.einsum('bhqk,bkhd->bqhd', prob_bf.astype(f32), values.astype(f32))).reshape(block_rows, D)
        total_one = x_block.astype(f32) + (jnp.dot(context, w_out, preferred_element_type=f32) + out_bias)
        attn_act, normed_one, inverse_one = norm_fwd(total_one, norm_gain, norm_shift)
        attn_bf = attn_act.astype(jnp.bfloat16)
        up_pre = jnp.dot(attn_bf, w_up, preferred_element_type=f32) + up_bias
        act_f, slope = gelu_parts(up_pre)
        act = act_f.astype(jnp.bfloat16)
        total_two = attn_act + (jnp.dot(act, w_down, preferred_element_type=f32) + down_bias)
        final, normed_two, inverse_two = norm_fwd(total_two, final_gain, final_shift)
        layer_out = final.astype(jnp.bfloat16)
        grad_top = g_block.astype(f32)
        fgain_part = lax.optimization_barrier(jnp.sum(grad_top * normed_two, axis=0))
        fshift_part = lax.optimization_barrier(jnp.sum(grad_top, axis=0))
        back_two = norm_bwd(grad_top, normed_two, inverse_two, final_gain)
        back_two_bf = back_two.astype(jnp.bfloat16)
        wdown_part = jnp.dot(act.T, back_two_bf, preferred_element_type=f32)
        dbias_part = lax.optimization_barrier(jnp.sum(back_two, axis=0))
        up_back = jnp.dot(back_two_bf, w_down.T, preferred_element_type=f32) * slope
        up_back_bf = up_back.astype(jnp.bfloat16)
        wup_part = jnp.dot(attn_bf.T, up_back_bf, preferred_element_type=f32)
        ubias_part = lax.optimization_barrier(jnp.sum(up_back, axis=0))
        attn_back = back_two + jnp.dot(up_back_bf, w_up.T, preferred_element_type=f32)
        ngain_part = lax.optimization_barrier(jnp.sum(attn_back * normed_one, axis=0))
        nshift_part = lax.optimization_barrier(jnp.sum(attn_back, axis=0))
        back_one = norm_bwd(attn_back, normed_one, inverse_one, norm_gain)
        back_one_bf = back_one.astype(jnp.bfloat16)
        wout_part = jnp.dot(context.T, back_one_bf, preferred_element_type=f32)
        obias_part = lax.optimization_barrier(jnp.sum(back_one, axis=0))
        ctx_back = rounded(jnp.dot(back_one_bf, w_out.T, preferred_element_type=f32)).reshape(group_seqs, LEN, HEADS, HD)
        v_back = jnp.einsum('bhqk,bqhd->bkhd', prob_bf.astype(f32), ctx_back.astype(f32))
        d_prob = jnp.einsum('bqhd,bkhd->bhqk', ctx_back.astype(f32), values.astype(f32))
        row_delta = lax.optimization_barrier(jnp.sum(prob_f * d_prob, axis=-1, keepdims=True))
        score_back = rounded(prob_f * (d_prob - row_delta) * score_scale)
        q_back = jnp.einsum('bhqk,bkhd->bqhd', score_back.astype(f32), keys.astype(f32)).reshape(block_rows, D)
        k_back = jnp.einsum('bhqk,bqhd->bkhd', score_back.astype(f32), query.astype(f32)).reshape(block_rows, D)
        v_back = v_back.reshape(block_rows, D)
        qkv_back = jnp.stack([q_back, k_back, v_back], axis=1).astype(jnp.bfloat16).reshape(block_rows, 3 * D)
        wqkv_part = jnp.dot(x_block.T, qkv_back, preferred_element_type=f32).reshape(D, 3, D)
        qbias_part = lax.optimization_barrier(jnp.sum(q_back, axis=0))
        vbias_part = lax.optimization_barrier(jnp.sum(v_back, axis=0))
        hidden_grad = back_one + jnp.dot(qkv_back, wq_flat.T, preferred_element_type=f32)
        grad_parts = (wqkv_part, qbias_part, vbias_part, wout_part, obias_part, ngain_part, nshift_part, wup_part, ubias_part, wdown_part, dbias_part, fgain_part, fshift_part)
        updated = tuple((old_sum + new_part for old_sum, new_part in zip(running, grad_parts)))
        return (updated, (layer_out, hidden_grad))
    zero_sums = (jnp.zeros((D, 3, D), f32), jnp.zeros((D,), f32), jnp.zeros((D,), f32), jnp.zeros((D, D), f32), jnp.zeros((D,), f32), jnp.zeros((D,), f32), jnp.zeros((D,), f32), jnp.zeros((D, FF), f32), jnp.zeros((FF,), f32), jnp.zeros((FF, D), f32), jnp.zeros((D,), f32), jnp.zeros((D,), f32), jnp.zeros((D,), f32))
    scanned = (hidden_in.reshape(block_count, block_rows, D), doc_ids.reshape(block_count, group_seqs, LEN), out_grad.reshape(block_count, block_rows, D))
    grad_sums, (outs_main, outs_grad) = lax.scan(block_step, zero_sums, scanned)
    return (outs_main.reshape(TOKENS, D), outs_grad.reshape(TOKENS, D), grad_sums[0], grad_sums[1], grad_sums[2], grad_sums[3], grad_sums[4], grad_sums[5], grad_sums[6], grad_sums[7], grad_sums[8], grad_sums[9], grad_sums[10], grad_sums[11], grad_sums[12])
```

```python
import functools

import jax
import jax.numpy as jnp
from jax import lax
from jax.experimental import pallas as pl
from jax.experimental.pallas import tpu as pltpu
from jax.sharding import PartitionSpec as P

HD = 64


EPS = 1e-12
INV_ROOT_TWO = 0.7071067811865476
INV_ROOT_PI = 0.3989422804014327


def gelu_parts(pre_act):
    cdf_val = 0.5 * (1.0 + lax.erf(pre_act * INV_ROOT_TWO))
    density = jnp.exp(-0.5 * pre_act * pre_act) * INV_ROOT_PI
    return (pre_act * cdf_val, cdf_val + pre_act * density)


def seq_scores(query, keys, doc_row):
    same_doc = doc_row[:, None] == doc_row[None, :]
    scores = jnp.einsum("qhd,khd->hqk", query, keys, preferred_element_type=jnp.float32) * HD ** (
        -0.5
    )
    return jnp.where(same_doc[None], scores, -jnp.inf)


def attend_seq(inputs_seq):
    query, keys, values, doc_row = inputs_seq
    scores = seq_scores(query, keys, doc_row)
    top_score = jnp.max(scores, axis=-1, keepdims=True)
    log_total = top_score + jnp.log(jnp.sum(jnp.exp(scores - top_score), axis=-1, keepdims=True))
    prob_bf = jnp.exp(scores - log_total).astype(jnp.bfloat16)
    context = jnp.einsum(
        "hqk,khd->qhd", prob_bf, values, preferred_element_type=jnp.float32
    ).astype(jnp.bfloat16)
    return (context, log_total)


def attend_back(inputs_seq):
    query, keys, values, doc_row, ctx_back, log_total = inputs_seq
    prob_f = jnp.exp(seq_scores(query, keys, doc_row) - log_total)
    v_back = jnp.einsum(
        "hqk,qhd->khd", prob_f.astype(jnp.bfloat16), ctx_back, preferred_element_type=jnp.float32
    )
    d_prob = jnp.einsum("qhd,khd->hqk", ctx_back, values, preferred_element_type=jnp.float32)
    row_delta = jnp.sum(prob_f * d_prob, axis=-1, keepdims=True)
    score_back = (prob_f * (d_prob - row_delta) * HD ** (-0.5)).astype(jnp.bfloat16)
    q_back = jnp.einsum("hqk,khd->qhd", score_back, keys, preferred_element_type=jnp.float32)
    k_back = jnp.einsum("hqk,qhd->khd", score_back, query, preferred_element_type=jnp.float32)
    return (q_back, k_back, v_back)


MESH = pl.DeviceIdType.MESH
VMEM = pl.BlockSpec(memory_space=pltpu.VMEM)
COST = pl.CostEstimate(flops=0, bytes_accessed=30_000_000, transcendentals=0)


def remote(src, dst, send_sem, recv_sem, target):
    return pltpu.make_async_remote_copy(
        src_ref=src,
        dst_ref=dst,
        send_sem=send_sem,
        recv_sem=recv_sem,
        device_id={"col": target},
        device_id_type=MESH,
    )


def place(count):
    me = lax.axis_index("col")
    chip, core = lax.div(me, 2), lax.rem(me, 2)
    return me, chip, core, chip * 2 + 1 - core


def greet(count, me):
    barrier = pltpu.get_barrier_semaphore()
    for step in range(1, count):
        pl.semaphore_signal(
            barrier,
            inc=1,
            device_id={"col": lax.rem(me + step, count)},
            device_id_type=MESH,
        )
    pl.semaphore_wait(barrier, count - 1)


def rows_of(index, size):
    return pl.ds(pl.multiple_of(index * size, size), size)


def start_reduce(count, view, slots, sums, s1, r1, s2, r2):
    me, chip, core, partner = place(count)
    chips = count // 2
    far = lambda step: lax.rem(chip + step, chips)
    order = list(range(1, chips)) + [0]
    first = {}
    for step in order:
        first[step] = remote(
            view(far(step) * 2 + 1 - core), slots.at[step], s1.at[step], r1.at[step], partner
        )
        first[step].start()
    second = {}
    for step in range(1, chips):
        first[step].wait_recv()
        owner = far(step) * 2 + core
        sums[step] = (
            view(owner)[...].astype(jnp.float32) + slots[step].astype(jnp.float32)
        ).astype(jnp.bfloat16)
        second[step] = remote(
            sums.at[step], sums.at[chips + step], s2.at[step], r2.at[step], owner
        )
        second[step].start()
    first[0].wait_recv()
    return first, second


def finish_reduce(count, view, slots, sums, pending):
    first, second = pending
    me = lax.axis_index("col")
    chips = count // 2
    total = view(me)[...].astype(jnp.float32) + slots[0].astype(jnp.float32)
    for step in range(1, chips):
        second[step].wait_recv()
        total = total + sums[chips + step].astype(jnp.float32)
    for copy in list(first.values()) + list(second.values()):
        copy.wait_send()
    return total


def gather_blocks(count, source, view, s3, r3, s4, r4):
    me, chip, core, partner = place(count)
    chips = count // 2
    sent = []
    for step in range(1, chips):
        peer = lax.rem(chip + step, chips) * 2 + core
        sent.append(remote(source, view(me), s3.at[step], r3.at[step], peer))
        sent[-1].start()
    near = remote(source, view(me), s3.at[0], r3.at[0], partner)
    near.start()
    return sent, near


def gather_rest(count, view, pending, s4, r4):
    me, chip, core, partner = place(count)
    chips = count // 2
    sent, near = pending
    passed = []
    for step in range(1, chips):
        origin = lax.rem(chip + chips - step, chips) * 2 + core
        sent[step - 1].wait_recv()
        passed.append(remote(view(origin), view(origin), s4.at[step], r4.at[step], partner))
        passed[-1].start()
    near.wait_recv()
    for copy in passed:
        copy.wait_recv()
    for copy in sent + [near] + passed:
        copy.wait_send()


def spread_kernel(count, x_ref, og_ref, par_ref, full_ref, og_out, par_out, *sems):
    s3, r3, s4, r4, sa, ra, sb, rb = sems
    me = lax.axis_index("col")
    width = x_ref.shape[1]
    rows = og_ref.shape[0] // count
    greet(count, me)
    view = lambda index: full_ref.at[:, rows_of(index, width)]
    pending = gather_blocks(count, x_ref, view, s3, r3, s4, r4)
    mine = rows_of(me, width)
    others = []
    for step in range(1, count):
        target = lax.rem(me + step, count)
        others.append(
            remote(og_ref.at[rows_of(target, rows), :], og_out.at[:, mine], sa.at[step], ra.at[step], target)
        )
        others.append(remote(par_ref, par_out.at[:, mine], sb.at[step], rb.at[step], target))
    for copy in others:
        copy.start()
    full_ref[:, mine] = x_ref[...]
    og_out[:, mine] = og_ref[rows_of(me, rows), :]
    par_out[:, mine] = par_ref[...]
    gather_rest(count, view, pending, s4, r4)
    for copy in others:
        copy.wait()


def spread_all(count, x, og, par):
    tokens, width = x.shape
    dma = pltpu.SemaphoreType.DMA
    return pl.pallas_call(
        functools.partial(spread_kernel, count),
        out_shape=(
            jax.ShapeDtypeStruct((tokens, width * count), x.dtype),
            jax.ShapeDtypeStruct((tokens // count, width * count), og.dtype),
            jax.ShapeDtypeStruct((par.shape[0], width * count), par.dtype),
        ),
        in_specs=[VMEM] * 3,
        out_specs=(VMEM,) * 3,
        scratch_shapes=[dma((count,))] * 8,
        compiler_params=pltpu.CompilerParams(collective_id=0, has_side_effects=True),
        cost_estimate=COST,
    )(x, og, par)


def middle_kernel(count, mid, n_aux, n_out, exchange, *refs):
    part = refs[0]
    aux = refs[1 : 1 + n_aux]
    full = refs[1 + n_aux]
    outs = refs[2 + n_aux : 2 + n_aux + n_out]
    slots, sums, swap, s1, r1, s2, r2, s3, r3, s4, r4, sa, ra = refs[2 + n_aux + n_out :]
    me = lax.axis_index("col")
    rows = part.shape[0] // count
    greet(count, me)
    view = lambda index: part.at[rows_of(index, rows), :]
    pending = start_reduce(count, view, slots, sums, s1, r1, s2, r2)
    total = finish_reduce(count, view, slots, sums, pending)
    mid(total, me, aux, outs, full.at[rows_of(me, rows), :], swap)
    out_view = lambda index: full.at[rows_of(index, rows), :]
    pending = gather_blocks(count, out_view(me), out_view, s3, r3, s4, r4)
    others = []
    if exchange:
        laid = outs[0]
        width = laid.shape[1]
        for step in range(1, count):
            target = lax.rem(me + step, count)
            others.append(
                remote(
                    swap.at[:, rows_of(target, width)],
                    laid.at[rows_of(me, rows), :],
                    sa.at[step],
                    ra.at[step],
                    target,
                )
            )
            others[-1].start()
        laid[rows_of(me, rows), :] = swap[:, rows_of(me, width)]
    gather_rest(count, out_view, pending, s4, r4)
    for copy in others:
        copy.wait()


def middle(count, part, aux, mid, outs, exchange, cid):
    tokens, width = part.shape
    rows = tokens // count
    dma = pltpu.SemaphoreType.DMA
    return pl.pallas_call(
        functools.partial(middle_kernel, count, mid, len(aux), len(outs), exchange),
        out_shape=(jax.ShapeDtypeStruct((tokens, width), jnp.bfloat16),) + tuple(outs),
        in_specs=[VMEM] * (1 + len(aux)),
        out_specs=(VMEM,) * (1 + len(outs)),
        scratch_shapes=[
            pltpu.VMEM((count // 2, rows, width), jnp.bfloat16),
            pltpu.VMEM((count, rows, width), jnp.bfloat16),
            pltpu.VMEM((rows, width), jnp.bfloat16),
        ]
        + [dma((count,))] * 10,
        compiler_params=pltpu.CompilerParams(collective_id=cid, has_side_effects=True),
        cost_estimate=COST,
    )(part, *aux)


def last_kernel(count, part, back_full, out, slots, sums, s1, r1, s2, r2):
    me = lax.axis_index("col")
    width = part.shape[1] // count
    greet(count, me)
    view = lambda index: part.at[:, rows_of(index, width)]
    pending = start_reduce(count, view, slots, sums, s1, r1, s2, r2)
    total = finish_reduce(count, view, slots, sums, pending)
    out[...] = total + back_full[:, rows_of(me, width)].astype(jnp.float32)


def last(count, part, back_full):
    tokens, width = part.shape
    cols = width // count
    dma = pltpu.SemaphoreType.DMA
    return pl.pallas_call(
        functools.partial(last_kernel, count),
        out_shape=jax.ShapeDtypeStruct((tokens, cols), jnp.float32),
        in_specs=[VMEM] * 2,
        out_specs=VMEM,
        scratch_shapes=[
            pltpu.VMEM((count // 2, tokens, cols), jnp.bfloat16),
            pltpu.VMEM((count, tokens, cols), jnp.bfloat16),
        ]
        + [dma((count,))] * 4,
        compiler_params=pltpu.CompilerParams(collective_id=4, has_side_effects=True),
        cost_estimate=COST,
    )(part, back_full)


def norm_parts(total):
    mean_val = jnp.mean(total, axis=1, keepdims=True)
    centered = total - mean_val
    inverse = lax.rsqrt(jnp.mean(centered * centered, axis=1, keepdims=True) + EPS)
    return centered * inverse, inverse


def norm_back(upstream, normed, inverse, gain):
    scaled = upstream * gain
    first = jnp.mean(scaled, axis=1, keepdims=True)
    second = jnp.mean(scaled * normed, axis=1, keepdims=True)
    return inverse * (scaled - first - normed * second)


def column_sum(values):
    return jnp.sum(values, axis=0, keepdims=True)


def mid_one(total, me, aux, outs, block, swap):
    x_full, par = aux
    act_out, normed_out, inverse_out = outs
    rows = total.shape[0]
    total = x_full[rows_of(me, rows), :].astype(jnp.float32) + (total + par[0:1, :])
    normed, inverse = norm_parts(total)
    act = normed * par[1:2, :] + par[2:3, :]
    act_out[...] = act
    normed_out[...] = normed
    inverse_out[...] = jnp.broadcast_to(inverse, inverse_out.shape)
    block[...] = act.astype(jnp.bfloat16)


def mid_two(total, me, aux, outs, block, swap):
    act, grad, par = aux
    laid, back_out, sum_out = outs
    total = act[...] + (total + par[3:4, :])
    normed, inverse = norm_parts(total)
    gain = par[4:5, :]
    swap[...] = (normed * gain + par[5:6, :]).astype(jnp.bfloat16)
    top = grad[...].astype(jnp.float32)
    back = norm_back(top, normed, inverse, gain)
    back_out[...] = back
    sum_out[0:1, :] = column_sum(top * normed)
    sum_out[1:2, :] = column_sum(top)
    sum_out[2:3, :] = column_sum(back)
    block[...] = back.astype(jnp.bfloat16)


def mid_three(total, me, aux, outs, block, swap):
    back_two, normed_ref, inverse, par = aux
    (sum_out,) = outs
    upstream = back_two[...] + total
    normed = normed_ref[...]
    back = norm_back(upstream, normed, inverse[:, 0:1], par[1:2, :])
    sum_out[0:1, :] = column_sum(upstream * normed)
    sum_out[1:2, :] = column_sum(upstream)
    sum_out[2:3, :] = column_sum(back)
    block[...] = back.astype(jnp.bfloat16)


def ring_gather(block, axis, count):
    me = lax.axis_index("row")
    ring = [(i, (i + 1) % count) for i in range(count)]
    size = block.shape[axis]
    shape = list(block.shape)
    shape[axis] = size * count
    whole = jnp.zeros(shape, block.dtype)
    for step in range(count):
        whole = lax.dynamic_update_slice_in_dim(
            whole, block, lax.rem(me - step + count, count) * size, axis
        )
        if step < count - 1:
            block = lax.ppermute(block, "row", ring)
    return whole


def ring_scatter(part, axis, count):
    me = lax.axis_index("row")
    ring = [(i, (i + 1) % count) for i in range(count)]
    size = part.shape[axis] // count

    def own(step):
        owner = lax.rem(me - 1 - step + 2 * count, count)
        return lax.dynamic_slice_in_dim(part, owner * size, size, axis)

    total = own(0).astype(jnp.bfloat16)
    for step in range(1, count):
        moved = lax.ppermute(total, "row", ring)
        total = (moved.astype(jnp.float32) + own(step).astype(jnp.float32)).astype(jnp.bfloat16)
    return total


def pair_sum(total, count):
    result = total.astype(jnp.float32)
    moved = total
    ring = [(i, (i + 1) % count) for i in range(count)]
    if count == 2:
        return result + lax.ppermute(moved, "dp", ring).astype(jnp.float32)
    return lax.psum(total, "dp").astype(jnp.float32)


def per_device(
    rows_n,
    cols_n,
    dp_n,
    hidden_in,
    doc_ids,
    w_qkv,
    query_bias,
    value_bias,
    w_out,
    out_bias,
    norm_gain,
    norm_shift,
    w_up,
    up_bias,
    w_down,
    down_bias,
    final_gain,
    final_shift,
    out_grad,
):
    f32 = jnp.float32
    bf16 = jnp.bfloat16
    tokens_dev = hidden_in.shape[0]
    col_width = hidden_in.shape[1]
    head_count = col_width // HD
    seq_count = doc_ids.shape[0]
    seq_len = doc_ids.shape[1]
    head_shape = (seq_count, seq_len, head_count, HD)
    width = col_width * cols_n
    part_rows = tokens_dev // cols_n
    qkv_full = ring_gather(w_qkv.reshape(w_qkv.shape[0], -1), 0, rows_n)
    out_full = ring_gather(w_out, 1, rows_n)
    up_full = ring_gather(w_up, 0, rows_n)
    down_full = ring_gather(w_down, 1, rows_n)
    blank = jnp.zeros_like(out_bias)
    par = jnp.stack(
        [out_bias, norm_gain, norm_shift, down_bias, final_gain, final_shift, blank, blank]
    )
    x_full, top_rows, par_full = spread_all(cols_n, hidden_in, out_grad, par)
    projected = jnp.dot(x_full, qkv_full, preferred_element_type=f32)
    query = (projected[:, :col_width] + query_bias).astype(bf16).reshape(head_shape)
    keys = projected[:, col_width : 2 * col_width].astype(bf16).reshape(head_shape)
    values = (projected[:, 2 * col_width :] + value_bias).astype(bf16).reshape(head_shape)
    context, log_total = lax.map(attend_seq, (query, keys, values, doc_ids))
    ctx_rows = context.reshape(tokens_dev, col_width)
    block_f32 = jax.ShapeDtypeStruct((part_rows, width), f32)
    sums_f32 = jax.ShapeDtypeStruct((8, width), f32)
    attn_full, attn_act, normed_one, inverse_one = middle(
        cols_n,
        jnp.dot(ctx_rows, out_full, preferred_element_type=f32).astype(bf16),
        (x_full, par_full),
        mid_one,
        (block_f32, block_f32, jax.ShapeDtypeStruct((part_rows, 128), f32)),
        False,
        1,
    )
    up_pre = jnp.dot(attn_full, up_full, preferred_element_type=f32) + up_bias
    act_f, slope = gelu_parts(up_pre)
    act = act_f.astype(bf16)
    back_two_full, layer_out, back_two, sums_two = middle(
        cols_n,
        jnp.dot(act, down_full, preferred_element_type=f32).astype(bf16),
        (attn_act, top_rows, par_full),
        mid_two,
        (jax.ShapeDtypeStruct((tokens_dev, col_width), bf16), block_f32, sums_f32),
        True,
        2,
    )
    up_back = jnp.dot(back_two_full, down_full.T, preferred_element_type=f32) * slope
    up_back_bf = up_back.astype(bf16)
    back_one_full, sums_one = middle(
        cols_n,
        jnp.dot(up_back_bf, up_full.T, preferred_element_type=f32).astype(bf16),
        (back_two, normed_one, inverse_one, par_full),
        mid_three,
        (sums_f32,),
        False,
        3,
    )
    wdown_part = jnp.dot(act.T, back_two_full, preferred_element_type=f32).astype(bf16)
    wdown_grad = pair_sum(ring_scatter(wdown_part, 1, rows_n), dp_n)
    wup_part = jnp.dot(attn_full.T, up_back_bf, preferred_element_type=f32).astype(bf16)
    wup_grad = pair_sum(ring_scatter(wup_part, 0, rows_n), dp_n)
    ubias_part = jnp.sum(up_back, axis=0)
    wout_part = jnp.dot(ctx_rows.T, back_one_full, preferred_element_type=f32).astype(bf16)
    wout_grad = pair_sum(ring_scatter(wout_part, 1, rows_n), dp_n)
    ctx_back = (
        jnp.dot(back_one_full, out_full.T, preferred_element_type=f32)
        .astype(bf16)
        .reshape(head_shape)
    )
    q_back, k_back, v_back = lax.map(
        attend_back, (query, keys, values, doc_ids, ctx_back, log_total)
    )
    q_back = q_back.reshape(tokens_dev, col_width)
    k_back = k_back.reshape(tokens_dev, col_width)
    v_back = v_back.reshape(tokens_dev, col_width)
    qbias_part = jnp.sum(q_back, axis=0)
    vbias_part = jnp.sum(v_back, axis=0)
    qkv_back = jnp.concatenate([q_back.astype(bf16), k_back.astype(bf16), v_back.astype(bf16)], axis=1)
    wqkv_part = jnp.dot(x_full.T, qkv_back, preferred_element_type=f32).astype(bf16)
    wqkv_grad = pair_sum(ring_scatter(wqkv_part, 0, rows_n), dp_n).reshape(w_qkv.shape)
    hidden_grad = last(
        cols_n,
        jnp.dot(qkv_back, qkv_full.T, preferred_element_type=f32).astype(bf16),
        back_one_full,
    )
    six = lax.psum(jnp.concatenate([sums_two[:3], sums_one[:3]], axis=0), ("dp", "row", "col"))
    six = lax.dynamic_slice_in_dim(six, lax.axis_index("col") * col_width, col_width, 1)
    local = lax.psum(jnp.concatenate([ubias_part, qbias_part, vbias_part]), ("dp", "row"))
    hidden_w = ubias_part.shape[0]
    return (
        layer_out,
        hidden_grad,
        wqkv_grad,
        local[hidden_w : hidden_w + col_width],
        local[hidden_w + col_width :],
        wout_grad,
        six[5],
        six[3],
        six[4],
        wup_grad,
        local[:hidden_w],
        wdown_grad,
        six[2],
        six[0],
        six[1],
    )


def solution(mesh):
    placed = (
        P(("dp", "row"), "col"),
        P(("dp", "row"), None),
        P("row", None, "col"),
        P("col"),
        P("col"),
        P("col", "row"),
        P("col"),
        P("col"),
        P("col"),
        P("row", "col"),
        P("col"),
        P("col", "row"),
        P("col"),
        P("col"),
        P("col"),
        P(("dp", "row"), "col"),
    )
    return jax.shard_map(
        functools.partial(per_device, mesh.shape["row"], mesh.shape["col"], mesh.shape["dp"]),
        mesh=mesh,
        in_specs=placed,
        out_specs=(
            P(("dp", "row"), "col"),
            P(("dp", "row"), "col"),
            P("row", None, "col"),
            P("col"),
            P("col"),
            P("col", "row"),
            P("col"),
            P("col"),
            P("col"),
            P("row", "col"),
            P("col"),
            P("col", "row"),
            P("col"),
            P("col"),
            P("col"),
        ),
        check_vma=False,
    )
```

```python
import functools

import jax
import jax.numpy as jnp
from jax import lax
from jax.experimental import pallas as pl
from jax.experimental.pallas import tpu as pltpu
from jax.sharding import PartitionSpec as P


HD = 64


EPS = 1e-12
INV_ROOT_TWO = 0.7071067811865476
INV_ROOT_PI = 0.3989422804014327


def gelu_parts(pre_act):
    cdf_val = 0.5 * (1.0 + lax.erf(pre_act * INV_ROOT_TWO))
    density = jnp.exp(-0.5 * pre_act * pre_act) * INV_ROOT_PI
    return (pre_act * cdf_val, cdf_val + pre_act * density)


def seq_scores(query, keys, doc_row):
    same_doc = doc_row[:, None] == doc_row[None, :]
    scores = jnp.einsum("qhd,khd->hqk", query, keys, preferred_element_type=jnp.float32) * HD ** (
        -0.5
    )
    return jnp.where(same_doc[None], scores, -jnp.inf)


def attend_seq(inputs_seq):
    query, keys, values, doc_row = inputs_seq
    scores = seq_scores(query, keys, doc_row)
    top_score = jnp.max(scores, axis=-1, keepdims=True)
    log_total = top_score + jnp.log(jnp.sum(jnp.exp(scores - top_score), axis=-1, keepdims=True))
    prob_bf = jnp.exp(scores - log_total).astype(jnp.bfloat16)
    context = jnp.einsum(
        "hqk,khd->qhd", prob_bf, values, preferred_element_type=jnp.float32
    ).astype(jnp.bfloat16)
    return (context, log_total)


def attend_back(inputs_seq):
    query, keys, values, doc_row, ctx_back, log_total = inputs_seq
    prob_f = jnp.exp(seq_scores(query, keys, doc_row) - log_total)
    v_back = jnp.einsum(
        "hqk,qhd->khd", prob_f.astype(jnp.bfloat16), ctx_back, preferred_element_type=jnp.float32
    )
    d_prob = jnp.einsum("qhd,khd->hqk", ctx_back, values, preferred_element_type=jnp.float32)
    row_delta = jnp.sum(prob_f * d_prob, axis=-1, keepdims=True)
    score_back = (prob_f * (d_prob - row_delta) * HD ** (-0.5)).astype(jnp.bfloat16)
    q_back = jnp.einsum("hqk,khd->qhd", score_back, keys, preferred_element_type=jnp.float32)
    k_back = jnp.einsum("hqk,qhd->khd", score_back, query, preferred_element_type=jnp.float32)
    return (q_back, k_back, v_back)


MESH = pl.DeviceIdType.MESH
VMEM = pl.BlockSpec(memory_space=pltpu.VMEM)
COST = pl.CostEstimate(flops=0, bytes_accessed=30_000_000, transcendentals=0)


def remote(src, dst, send_sem, recv_sem, target):
    return pltpu.make_async_remote_copy(
        src_ref=src,
        dst_ref=dst,
        send_sem=send_sem,
        recv_sem=recv_sem,
        device_id={"col": target},
        device_id_type=MESH,
    )


def place():
    me = lax.axis_index("col")
    chip, core = lax.div(me, 2), lax.rem(me, 2)
    return me, chip, core, chip * 2 + 1 - core


def greet(count, me, rows_n=1, dp_n=1):
    barrier = pltpu.get_barrier_semaphore()
    targets = [{"col": lax.rem(me + step, count)} for step in range(1, count)]
    if rows_n > 1:
        row = lax.axis_index("row")
        targets.append({"row": lax.rem(row + 1, rows_n)})
        targets.append({"row": lax.rem(row + rows_n - 1, rows_n)})
        dp = lax.axis_index("dp")
        targets += [{"dp": lax.rem(dp + step, dp_n)} for step in range(1, dp_n)]
    for target in targets:
        pl.semaphore_signal(barrier, inc=1, device_id=target, device_id_type=MESH)
    pl.semaphore_wait(barrier, len(targets))


def rows_of(index, size):
    return pl.ds(pl.multiple_of(index * size, size), size)


def row_view(axis, shape, dp_n):
    share = shape[0] // dp_n
    if axis == 0:
        return lambda ref, index, part: ref.at[
            pl.ds(pl.multiple_of(index * shape[0] + part * share, share), share), :
        ]
    if shape[1] % 128 == 0:
        return lambda ref, index, part: ref.at[
            pl.ds(pl.multiple_of(part * share, share), share), rows_of(index, shape[1])
        ]
    return lambda ref, index, part: ref.at[
        index, pl.ds(pl.multiple_of(part * share, share), share), :
    ]


def full_shape(axis, shape, rows_n):
    if axis == 0:
        return (shape[0] * rows_n, shape[1])
    if shape[1] % 128 == 0:
        return (shape[0], shape[1] * rows_n)
    return (rows_n,) + tuple(shape)


def unstack(whole):
    if whole.ndim == 2:
        return whole
    return jnp.moveaxis(whole, 0, 1).reshape(whole.shape[1], -1)


def weight_ring(rows_n, dp_n, block, whole, axis, sems):
    zs, zr, xs, xr = sems
    row, dp = lax.axis_index("row"), lax.axis_index("dp")
    view = row_view(axis, block.shape, dp_n)
    share = block.shape[0] // dp_n
    after = lax.rem(row + 1, rows_n)
    started = []

    def start(src, dst, send, recv, target):
        copy = pltpu.make_async_remote_copy(
            src_ref=src, dst_ref=dst, send_sem=send, recv_sem=recv,
            device_id=target, device_id_type=MESH,
        )
        copy.start()
        started.append(copy)
        return copy

    source = block.at[pl.ds(pl.multiple_of(dp * share, share), share), :]
    moving = start(source, view(whole, row, dp), zs.at[0], zr.at[0], {"row": after})
    for part in range(dp_n):
        view(whole, row, part)[...] = block[pl.ds(part * share, share), :]
    swaps = []
    yield
    for step in range(rows_n - 1):
        moving.wait_recv()
        here = view(whole, lax.rem(row - 1 - step + rows_n, rows_n), dp)
        if step < rows_n - 2:
            moving = start(here, here, zs.at[step + 1], zr.at[step + 1], {"row": after})
        for other in range(1, dp_n):
            slot = step * dp_n + other
            swaps.append(
                start(here, here, xs.at[slot], xr.at[slot], {"dp": lax.rem(dp + other, dp_n)})
            )
        yield
    for copy in swaps:
        copy.wait_recv()
    for copy in started:
        copy.wait_send()


def ring_sems(rows_n, dp_n):
    dma = pltpu.SemaphoreType.DMA
    return [dma((rows_n,)), dma((rows_n,)), dma((rows_n * dp_n,)), dma((rows_n * dp_n,))]


def advance(rings):
    for ring in rings:
        next(ring, None)


def start_reduce(count, view, slots, sums, s1, r1, s2, r2):
    _, chip, core, partner = place()
    chips = count // 2
    far = lambda step: lax.rem(chip + step, chips)
    order = list(range(1, chips)) + [0]
    first = {}
    for step in order:
        first[step] = remote(
            view(far(step) * 2 + 1 - core), slots.at[step], s1.at[step], r1.at[step], partner
        )
        first[step].start()
    second = {}
    for step in range(1, chips):
        first[step].wait_recv()
        owner = far(step) * 2 + core
        sums[step] = (
            view(owner)[...].astype(jnp.float32) + slots[step].astype(jnp.float32)
        ).astype(jnp.bfloat16)
        second[step] = remote(
            sums.at[step], sums.at[chips + step], s2.at[step], r2.at[step], owner
        )
        second[step].start()
    first[0].wait_recv()
    return first, second


def finish_reduce(count, view, slots, sums, pending):
    first, second = pending
    me = lax.axis_index("col")
    chips = count // 2
    total = view(me)[...].astype(jnp.float32) + slots[0].astype(jnp.float32)
    for step in range(1, chips):
        second[step].wait_recv()
        total = total + sums[chips + step].astype(jnp.float32)
    for copy in list(first.values()) + list(second.values()):
        copy.wait_send()
    return total


def gather_blocks(count, source, view, s3, r3):
    me, chip, core, partner = place()
    chips = count // 2
    sent = []
    for step in range(1, chips):
        peer = lax.rem(chip + step, chips) * 2 + core
        sent.append(remote(source, view(me), s3.at[step], r3.at[step], peer))
        sent[-1].start()
    near = remote(source, view(me), s3.at[0], r3.at[0], partner)
    near.start()
    return sent, near


def gather_rest(count, view, pending, s4, r4):
    _, chip, core, partner = place()
    chips = count // 2
    sent, near = pending
    passed = []
    for step in range(1, chips):
        origin = lax.rem(chip + chips - step, chips) * 2 + core
        sent[step - 1].wait_recv()
        passed.append(remote(view(origin), view(origin), s4.at[step], r4.at[step], partner))
        passed[-1].start()
    near.wait_recv()
    for copy in passed:
        copy.wait_recv()
    for copy in sent + [near] + passed:
        copy.wait_send()


def spread_kernel(count, rows_n, dp_n, axes, *refs):
    n = len(axes)
    x_ref, og_ref, par_ref = refs[:3]
    blocks = refs[3 : 3 + n]
    full_ref, og_out, par_out = refs[3 + n : 6 + n]
    wholes = refs[6 + n : 6 + 2 * n]
    sems = refs[6 + 2 * n :]
    s3, r3, s4, r4, sa, ra, sb, rb = sems[:8]
    me = lax.axis_index("col")
    width = x_ref.shape[1]
    rows = og_ref.shape[0] // count
    greet(count, me, rows_n, dp_n)
    rings = [
        weight_ring(rows_n, dp_n, blocks[i], wholes[i], axes[i], sems[8 + 4 * i : 12 + 4 * i])
        for i in range(n)
    ]
    advance(rings)
    view = lambda index: full_ref.at[:, rows_of(index, width)]
    pending = gather_blocks(count, x_ref, view, s3, r3)
    mine = rows_of(me, width)
    others = []
    for step in range(1, count):
        target = lax.rem(me + step, count)
        others.append(
            remote(og_ref.at[rows_of(target, rows), :], og_out.at[:, mine], sa.at[step], ra.at[step], target)
        )
        others.append(remote(par_ref, par_out.at[:, mine], sb.at[step], rb.at[step], target))
    for copy in others:
        copy.start()
    full_ref[:, mine] = x_ref[...]
    og_out[:, mine] = og_ref[rows_of(me, rows), :]
    par_out[:, mine] = par_ref[...]
    advance(rings)
    gather_rest(count, view, pending, s4, r4)
    for _ in range(rows_n):
        advance(rings)
    for copy in others:
        copy.wait()


def spread_all(count, rows_n, dp_n, x, og, par, blocks, axes):
    tokens, width = x.shape
    dma = pltpu.SemaphoreType.DMA
    return pl.pallas_call(
        functools.partial(spread_kernel, count, rows_n, dp_n, axes),
        out_shape=(
            jax.ShapeDtypeStruct((tokens, width * count), x.dtype),
            jax.ShapeDtypeStruct((tokens // count, width * count), og.dtype),
            jax.ShapeDtypeStruct((par.shape[0], width * count), par.dtype),
        )
        + tuple(
            jax.ShapeDtypeStruct(full_shape(axis, block.shape, rows_n), block.dtype)
            for axis, block in zip(axes, blocks)
        ),
        in_specs=[VMEM] * (3 + len(blocks)),
        out_specs=(VMEM,) * (3 + len(blocks)),
        scratch_shapes=[dma((count,))] * 8 + ring_sems(rows_n, dp_n) * len(blocks),
        compiler_params=pltpu.CompilerParams(collective_id=0, has_side_effects=True),
        cost_estimate=COST,
    )(x, og, par, *blocks)


def middle_kernel(count, mid, n_aux, n_out, exchange, ring_of, *refs):
    part = refs[0]
    rings = []
    if ring_of is not None:
        rows_n, dp_n, axis = ring_of
        n_aux, n_out = n_aux + 1, n_out + 1
    aux = refs[1 : 1 + n_aux]
    full = refs[1 + n_aux]
    outs = refs[2 + n_aux : 2 + n_aux + n_out]
    slots, sums, swap, s1, r1, s2, r2, s3, r3, s4, r4, sa, ra = refs[2 + n_aux + n_out :][:13]
    me = lax.axis_index("col")
    rows = part.shape[0] // count
    if ring_of is None:
        greet(count, me)
    else:
        greet(count, me, rows_n, dp_n)
        rings.append(
            weight_ring(rows_n, dp_n, aux[-1], outs[-1], axis, refs[2 + n_aux + n_out :][13:])
        )
        aux, outs = aux[:-1], outs[:-1]
    advance(rings)
    view = lambda index: part.at[rows_of(index, rows), :]
    pending = start_reduce(count, view, slots, sums, s1, r1, s2, r2)
    advance(rings)
    total = finish_reduce(count, view, slots, sums, pending)
    mid(total, me, aux, outs, full.at[rows_of(me, rows), :], swap)
    out_view = lambda index: full.at[rows_of(index, rows), :]
    pending = gather_blocks(count, out_view(me), out_view, s3, r3)
    others = []
    if exchange:
        laid = outs[0]
        width = laid.shape[1]
        for step in range(1, count):
            target = lax.rem(me + step, count)
            others.append(
                remote(
                    swap.at[:, rows_of(target, width)],
                    laid.at[rows_of(me, rows), :],
                    sa.at[step],
                    ra.at[step],
                    target,
                )
            )
            others[-1].start()
        laid[rows_of(me, rows), :] = swap[:, rows_of(me, width)]
    advance(rings)
    gather_rest(count, out_view, pending, s4, r4)
    if rings:
        for _ in range(rows_n):
            advance(rings)
    for copy in others:
        copy.wait()


def middle(count, part, aux, mid, outs, exchange, cid, ring_of=None, block=None):
    body = functools.partial(
        middle_kernel, count, mid, len(aux), len(outs), exchange, ring_of
    )
    extra = []
    if ring_of is not None:
        rows_n, dp_n, axis = ring_of
        aux = tuple(aux) + (block,)
        outs = tuple(outs) + (
            jax.ShapeDtypeStruct(full_shape(axis, block.shape, rows_n), block.dtype),
        )
        extra = ring_sems(rows_n, dp_n)
    tokens, width = part.shape
    rows = tokens // count
    dma = pltpu.SemaphoreType.DMA
    return middle_call(body, tokens, width, outs, aux, count, rows, dma, extra, cid, part)


def middle_call(body, tokens, width, outs, aux, count, rows, dma, extra, cid, part):
    return pl.pallas_call(
        body,
        out_shape=(jax.ShapeDtypeStruct((tokens, width), jnp.bfloat16),) + tuple(outs),
        in_specs=[VMEM] * (1 + len(aux)),
        out_specs=(VMEM,) * (1 + len(outs)),
        scratch_shapes=[
            pltpu.VMEM((count // 2, rows, width), jnp.bfloat16),
            pltpu.VMEM((count, rows, width), jnp.bfloat16),
            pltpu.VMEM((rows, width), jnp.bfloat16),
        ]
        + [dma((count,))] * 10
        + extra,
        compiler_params=pltpu.CompilerParams(collective_id=cid, has_side_effects=True),
        cost_estimate=COST,
    )(part, *aux)


def last_kernel(count, rows_n, dp_n, *refs):
    part, back_full, six_two, six_one, local, out, sums_out = refs[:7]
    slots, sums, gathered, packed, landed = refs[7:12]
    s1, r1, s2, r2, sa, ra, sb, rb = refs[12:]
    me = lax.axis_index("col")
    width = part.shape[1] // count
    row, dp = lax.axis_index("row"), lax.axis_index("dp")
    peers = rows_n * dp_n
    mine = dp * rows_n + row
    barrier = pltpu.get_barrier_semaphore()

    def peer(step):
        index = lax.rem(mine + step, peers)
        return {"dp": lax.div(index, rows_n), "row": lax.rem(index, rows_n)}

    for step in range(1, count):
        target = {"col": lax.rem(me + step, count)}
        pl.semaphore_signal(barrier, inc=1, device_id=target, device_id_type=MESH)
    for step in range(1, peers):
        pl.semaphore_signal(barrier, inc=1, device_id=peer(step), device_id_type=MESH)
    pl.semaphore_wait(barrier, count + peers - 2)
    view = lambda index: part.at[:, rows_of(index, width)]
    small = []
    for step in range(1, count):
        target = lax.rem(me + step, count)
        for which, ref in enumerate((six_two, six_one)):
            small.append(
                remote(
                    ref.at[:, rows_of(target, width)],
                    gathered.at[step, which],
                    sa.at[2 * step + which],
                    ra.at[2 * step + which],
                    target,
                )
            )
            small[-1].start()
    pending = start_reduce(count, view, slots, sums, s1, r1, s2, r2)
    for copy in small:
        copy.wait()
    for which, ref in enumerate((six_two, six_one)):
        total = ref[:, rows_of(me, width)]
        for step in range(1, count):
            total = total + gathered[step, which]
        packed[pl.ds(8 * which, 8), :] = total
    packed[pl.ds(16, local.shape[0]), :] = local[...]
    sent = []
    for step in range(1, peers):
        sent.append(
            pltpu.make_async_remote_copy(
                src_ref=packed,
                dst_ref=landed.at[mine],
                send_sem=sb.at[step],
                recv_sem=rb.at[step],
                device_id=peer(step),
                device_id_type=MESH,
            )
        )
        sent[-1].start()
    landed[mine] = packed[...]
    total = finish_reduce(count, view, slots, sums, pending)
    out[...] = total + back_full[:, rows_of(me, width)].astype(jnp.float32)
    for copy in sent:
        copy.wait()
    total = landed[0]
    for index in range(1, peers):
        total = total + landed[index]
    sums_out[...] = total


def last(count, rows_n, dp_n, part, back_full, six_two, six_one, local):
    tokens, width = part.shape
    cols = width // count
    dma = pltpu.SemaphoreType.DMA
    height = 16 + local.shape[0]
    peers = rows_n * dp_n
    return pl.pallas_call(
        functools.partial(last_kernel, count, rows_n, dp_n),
        out_shape=(
            jax.ShapeDtypeStruct((tokens, cols), jnp.float32),
            jax.ShapeDtypeStruct((height, cols), jnp.float32),
        ),
        in_specs=[VMEM] * 5,
        out_specs=(VMEM,) * 2,
        scratch_shapes=[
            pltpu.VMEM((count // 2, tokens, cols), jnp.bfloat16),
            pltpu.VMEM((count, tokens, cols), jnp.bfloat16),
            pltpu.VMEM((count, 2, 8, cols), jnp.float32),
            pltpu.VMEM((height, cols), jnp.float32),
            pltpu.VMEM((peers, height, cols), jnp.float32),
        ]
        + [dma((count,))] * 4
        + [dma((2 * count,))] * 2
        + [dma((peers,))] * 2,
        compiler_params=pltpu.CompilerParams(collective_id=4, has_side_effects=True),
        cost_estimate=COST,
    )(part, back_full, six_two, six_one, local)


def norm_parts(total):
    mean_val = jnp.mean(total, axis=1, keepdims=True)
    centered = total - mean_val
    inverse = lax.rsqrt(jnp.mean(centered * centered, axis=1, keepdims=True) + EPS)
    return centered * inverse, inverse


def norm_back(upstream, normed, inverse, gain):
    scaled = upstream * gain
    first = jnp.mean(scaled, axis=1, keepdims=True)
    second = jnp.mean(scaled * normed, axis=1, keepdims=True)
    return inverse * (scaled - first - normed * second)


def column_sum(values):
    return jnp.sum(values, axis=0, keepdims=True)


def mid_one(total, me, aux, outs, block, swap):
    x_full, par = aux
    act_out, normed_out, inverse_out = outs
    rows = total.shape[0]
    total = x_full[rows_of(me, rows), :].astype(jnp.float32) + (total + par[0:1, :])
    normed, inverse = norm_parts(total)
    act = normed * par[1:2, :] + par[2:3, :]
    act_out[...] = act
    normed_out[...] = normed
    inverse_out[...] = jnp.broadcast_to(inverse, inverse_out.shape)
    block[...] = act.astype(jnp.bfloat16)


def mid_two(total, me, aux, outs, block, swap):
    act, grad, par = aux
    _, back_out, sum_out = outs
    total = act[...] + (total + par[3:4, :])
    normed, inverse = norm_parts(total)
    gain = par[4:5, :]
    swap[...] = (normed * gain + par[5:6, :]).astype(jnp.bfloat16)
    top = grad[...].astype(jnp.float32)
    back = norm_back(top, normed, inverse, gain)
    back_out[...] = back
    sum_out[...] = jnp.zeros(sum_out.shape, jnp.float32)
    sum_out[0:1, :] = column_sum(top * normed)
    sum_out[1:2, :] = column_sum(top)
    sum_out[2:3, :] = column_sum(back)
    block[...] = back.astype(jnp.bfloat16)


def mid_three(total, me, aux, outs, block, swap):
    back_two, normed_ref, inverse, par = aux
    (sum_out,) = outs
    upstream = back_two[...] + total
    normed = normed_ref[...]
    back = norm_back(upstream, normed, inverse[:, 0:1], par[1:2, :])
    sum_out[...] = jnp.zeros(sum_out.shape, jnp.float32)
    sum_out[0:1, :] = column_sum(upstream * normed)
    sum_out[1:2, :] = column_sum(upstream)
    sum_out[2:3, :] = column_sum(back)
    block[...] = back.astype(jnp.bfloat16)


def ring_scatter(part, axis, count):
    me = lax.axis_index("row")
    ring = [(i, (i + 1) % count) for i in range(count)]
    size = part.shape[axis] // count

    def own(step):
        owner = lax.rem(me - 1 - step + 2 * count, count)
        return lax.dynamic_slice_in_dim(part, owner * size, size, axis)

    total = own(0).astype(jnp.bfloat16)
    for step in range(1, count):
        moved = lax.ppermute(total, "row", ring)
        total = (moved.astype(jnp.float32) + own(step).astype(jnp.float32)).astype(jnp.bfloat16)
    return total


def pair_sum(total, count):
    result = total.astype(jnp.float32)
    moved = total
    ring = [(i, (i + 1) % count) for i in range(count)]
    if count == 2:
        return result + lax.ppermute(moved, "dp", ring).astype(jnp.float32)
    return lax.psum(total, "dp").astype(jnp.float32)


def per_device(
    rows_n,
    cols_n,
    dp_n,
    hidden_in,
    doc_ids,
    w_qkv,
    query_bias,
    value_bias,
    w_out,
    out_bias,
    norm_gain,
    norm_shift,
    w_up,
    up_bias,
    w_down,
    down_bias,
    final_gain,
    final_shift,
    out_grad,
):
    f32 = jnp.float32
    bf16 = jnp.bfloat16
    tokens_dev = hidden_in.shape[0]
    col_width = hidden_in.shape[1]
    head_count = col_width // HD
    seq_count = doc_ids.shape[0]
    seq_len = doc_ids.shape[1]
    head_shape = (seq_count, seq_len, head_count, HD)
    width = col_width * cols_n
    part_rows = tokens_dev // cols_n
    blank = jnp.zeros_like(out_bias)
    par = jnp.stack(
        [out_bias, norm_gain, norm_shift, down_bias, final_gain, final_shift, blank, blank]
    )
    x_full, top_rows, par_full, qkv_full, out_full, up_full = spread_all(
        cols_n,
        rows_n,
        dp_n,
        hidden_in,
        out_grad,
        par,
        (w_qkv.reshape(w_qkv.shape[0], -1), w_out, w_up),
        (0, 1, 0),
    )
    out_full = unstack(out_full)
    projected = jnp.dot(x_full, qkv_full, preferred_element_type=f32)
    query = (projected[:, :col_width] + query_bias).astype(bf16).reshape(head_shape)
    keys = projected[:, col_width : 2 * col_width].astype(bf16).reshape(head_shape)
    values = (projected[:, 2 * col_width :] + value_bias).astype(bf16).reshape(head_shape)
    context, log_total = lax.map(attend_seq, (query, keys, values, doc_ids))
    ctx_rows = context.reshape(tokens_dev, col_width)
    block_f32 = jax.ShapeDtypeStruct((part_rows, width), f32)
    sums_f32 = jax.ShapeDtypeStruct((8, width), f32)
    attn_full, attn_act, normed_one, inverse_one, down_full = middle(
        cols_n,
        jnp.dot(ctx_rows, out_full, preferred_element_type=f32).astype(bf16),
        (x_full, par_full),
        mid_one,
        (block_f32, block_f32, jax.ShapeDtypeStruct((part_rows, 128), f32)),
        False,
        1,
        (rows_n, dp_n, 1),
        w_down,
    )
    down_full = unstack(down_full)
    up_pre = jnp.dot(attn_full, up_full, preferred_element_type=f32) + up_bias
    act_f, slope = gelu_parts(up_pre)
    act = act_f.astype(bf16)
    back_two_full, layer_out, back_two, sums_two = middle(
        cols_n,
        jnp.dot(act, down_full, preferred_element_type=f32).astype(bf16),
        (attn_act, top_rows, par_full),
        mid_two,
        (jax.ShapeDtypeStruct((tokens_dev, col_width), bf16), block_f32, sums_f32),
        True,
        2,
    )
    up_back = jnp.dot(back_two_full, down_full.T, preferred_element_type=f32) * slope
    up_back_bf = up_back.astype(bf16)
    back_one_full, sums_one = middle(
        cols_n,
        jnp.dot(up_back_bf, up_full.T, preferred_element_type=f32).astype(bf16),
        (back_two, normed_one, inverse_one, par_full),
        mid_three,
        (sums_f32,),
        False,
        3,
    )
    wdown_part = jnp.dot(act.T, back_two_full, preferred_element_type=f32).astype(bf16)
    wdown_grad = pair_sum(ring_scatter(wdown_part, 1, rows_n), dp_n)
    wup_part = jnp.dot(attn_full.T, up_back_bf, preferred_element_type=f32).astype(bf16)
    wup_grad = pair_sum(ring_scatter(wup_part, 0, rows_n), dp_n)
    ubias_part = jnp.sum(up_back, axis=0)
    wout_part = jnp.dot(ctx_rows.T, back_one_full, preferred_element_type=f32).astype(bf16)
    wout_grad = pair_sum(ring_scatter(wout_part, 1, rows_n), dp_n)
    ctx_back = jnp.dot(back_one_full, out_full.T, preferred_element_type=f32).astype(bf16)
    ctx_back = ctx_back.reshape(head_shape)
    q_back, k_back, v_back = lax.map(
        attend_back, (query, keys, values, doc_ids, ctx_back, log_total)
    )
    q_back = q_back.reshape(tokens_dev, col_width)
    k_back = k_back.reshape(tokens_dev, col_width)
    v_back = v_back.reshape(tokens_dev, col_width)
    qbias_part = jnp.sum(q_back, axis=0)
    vbias_part = jnp.sum(v_back, axis=0)
    qkv_back = jnp.concatenate([q_back.astype(bf16), k_back.astype(bf16), v_back.astype(bf16)], axis=1)
    wqkv_part = jnp.dot(x_full.T, qkv_back, preferred_element_type=f32).astype(bf16)
    wqkv_grad = pair_sum(ring_scatter(wqkv_part, 0, rows_n), dp_n).reshape(w_qkv.shape)
    local = jnp.concatenate([ubias_part, qbias_part, vbias_part])
    filled = -(-local.shape[0] // (8 * col_width)) * 8 * col_width
    local = jnp.pad(local, (0, filled - local.shape[0])).reshape(-1, col_width)
    hidden_part = jnp.dot(qkv_back, qkv_full.T, preferred_element_type=f32).astype(bf16)
    hidden_grad, sums = last(
        cols_n, rows_n, dp_n, hidden_part, back_one_full, sums_two, sums_one, local
    )
    local = sums[16:].reshape(-1)
    hidden_w = ubias_part.shape[0]
    return (
        layer_out,
        hidden_grad,
        wqkv_grad,
        local[hidden_w : hidden_w + col_width],
        local[hidden_w + col_width : hidden_w + 2 * col_width],
        wout_grad,
        sums[10],
        sums[8],
        sums[9],
        wup_grad,
        local[:hidden_w],
        wdown_grad,
        sums[2],
        sums[0],
        sums[1],
    )


def solution(mesh):
    placed = (
        P(("dp", "row"), "col"),
        P(("dp", "row"), None),
        P("row", None, "col"),
        P("col"),
        P("col"),
        P("col", "row"),
        P("col"),
        P("col"),
        P("col"),
        P("row", "col"),
        P("col"),
        P("col", "row"),
        P("col"),
        P("col"),
        P("col"),
        P(("dp", "row"), "col"),
    )
    return jax.shard_map(
        functools.partial(per_device, mesh.shape["row"], mesh.shape["col"], mesh.shape["dp"]),
        mesh=mesh,
        in_specs=placed,
        out_specs=(
            P(("dp", "row"), "col"),
            P(("dp", "row"), "col"),
            P("row", None, "col"),
            P("col"),
            P("col"),
            P("col", "row"),
            P("col"),
            P("col"),
            P("col"),
            P("row", "col"),
            P("col"),
            P("col", "row"),
            P("col"),
            P("col"),
            P("col"),
        ),
        check_vma=False,
    )
```
